32 devices in a mesh: row: 16 (over z, y, x), col: 2 (over core).
Axes of the slice: x: 2, y: 2, z: 4, core: 2. Of those that a mesh axis runs over, the one named last changes fastest.
Arguments:
- left_site: bfloat16 [384, 3, 4096], P('row'), may hold values from -6 to 6
- right_site: bfloat16 [4096, 3, 4096], P('row', None, 'col'), may hold values from -0.09375 to 0.09375
- gate: float32 [9, 9], replicated, may hold values from -2 to 2
- probes_matrix: bfloat16 [12288, 256], P('col'), may hold values from -0.0546875 to 0.0546875
Outputs:
- basis: float32 [1152, 256], P('row')
- new_block: float32 [256, 12288], P('row', 'col')
The draws below stay inside these ranges and needn't reach their ends.
All inputs are finite; a program needn't handle non-finite values.
Results may differ from the reference program's by a relative error of at most 0.0044.
Values may be sent and summed in bfloat16 or wider, within the bound.
A program may use at most 128 MiB of HBM per device.

```python
import jax
import jax.numpy as jnp
from jax import lax

CHI = 4096
CUTOFF = 3
A_DEV = 24
PROBES = 256
LEFT = 384
ORDER = 12288


def block_levels(own_key, dims, split, smallest, top_value):
    level = 1.0
    for axis_at, blocks in split:
        draws = jax.random.uniform(jax.random.fold_in(jax.random.fold_in(own_key, 6), axis_at), (blocks,), jnp.float32, smallest / len(split), top_value / len(split))
        level = level * jnp.repeat(jnp.exp(draws), dims[axis_at] // blocks).reshape((-1,) + (1,) * (len(dims) - 1 - axis_at))
    return level


def scatter_about(own_key, extent, deviation, most, split=(), kind=jnp.bfloat16):
    array = deviation * jax.random.normal(own_key, extent, jnp.float32)
    if split:
        array = array * block_levels(own_key, extent, split, -0.22, 0.18)
    return jnp.clip(array, -most, most).astype(kind)


def setup_inputs(seed: int = 0) -> dict:
    arg_keys = jax.random.split(jax.random.key(seed), 5)
    left_site = scatter_about(arg_keys[0], (LEFT, CUTOFF, CHI), 1.0, 6.0, ((0, 16),))
    right_site = scatter_about(arg_keys[1], (CHI, CUTOFF, CHI), CHI ** -0.5, 0.09375, ((0, 16), (2, 2)))
    gate = scatter_about(arg_keys[2], (CUTOFF * CUTOFF, CUTOFF * CUTOFF), (CUTOFF * CUTOFF) ** -0.5, 2.0, (), jnp.float32)
    probes_matrix = scatter_about(arg_keys[3], (ORDER, PROBES), ORDER ** -0.5, 0.0546875, ((0, 2),))
    return {"left_site": left_site, "right_site": right_site, "gate": gate, "probes_matrix": probes_matrix}


def reference(left_site, right_site, gate, probes_matrix):
    block_a = 4 * A_DEV
    right_cols = right_site.astype(jnp.float32).reshape(CHI, CUTOFF * CHI)
    gate_four = gate.reshape(CUTOFF, CUTOFF, CUTOFF, CUTOFF)
    left_blocks = left_site.astype(jnp.float32).reshape(LEFT // block_a, block_a * CUTOFF, CHI)
    probes_wide = probes_matrix.astype(jnp.float32)

    def step(carry, left_block):
        gram, projected = carry
        mixed = jnp.dot(left_block, right_cols)
        mixed = mixed.reshape(block_a, CUTOFF, CUTOFF, CHI)
        theta = jnp.einsum('stuv,auvb->asbt', gate_four, mixed, precision=lax.Precision.HIGHEST)
        theta = theta.reshape(block_a * CUTOFF, CHI * CUTOFF).astype(jnp.bfloat16)
        theta_wide = theta.astype(jnp.float32)
        sketch = jnp.dot(theta_wide, probes_wide).astype(jnp.bfloat16)
        sketch_wide = sketch.astype(jnp.float32)
        gram = gram + jnp.dot(sketch_wide.T, sketch_wide, precision=lax.Precision.HIGHEST)
        projected = projected + jnp.dot(sketch_wide.T, theta_wide, precision=lax.Precision.HIGHEST)
        return ((gram, projected), sketch)
    start = (jnp.zeros((PROBES, PROBES), jnp.float32), jnp.zeros((PROBES, CUTOFF * CHI), jnp.float32))
    (gram, projected), sketches = lax.scan(step, start, left_blocks)
    sketch_all = sketches.reshape(CUTOFF * LEFT, PROBES).astype(jnp.float32)
    factor = jnp.linalg.cholesky(gram)
    basis = lax.linalg.triangular_solve(factor, sketch_all, left_side=False, lower=True, transpose_a=True)
    new_block = lax.linalg.triangular_solve(factor, projected, left_side=True, lower=True)
    return (basis, new_block)
```

```python
import functools

import jax
import jax.numpy as jnp
from jax import lax
from jax.experimental import pallas as pl
from jax.experimental.pallas import tpu as pltpu
from jax.sharding import PartitionSpec as P

CUTOFF = 3
LANES = 128
GROUP = 4
HIGHEST = lax.Precision.HIGHEST


def dot(a, b, dims=((1,), (0,))):
    return lax.dot_general(a, b, (dims, ((), ())), preferred_element_type=jnp.float32)


def split(x):
    high = x.astype(jnp.bfloat16)
    low = (x - high.astype(jnp.float32)).astype(jnp.bfloat16)
    return high, low


def probe_kernel(gate_ref, right_ref, probes_ref, high_ref, low_ref, work_ref):
    width = probes_ref.shape[1] // CUTOFF
    for inner in range(CUTOFF):
        work_ref[inner] = dot(right_ref[inner], probes_ref[...])
    count_c = right_ref.shape[1]
    step = min(count_c, 64)
    for base in range(0, count_c, step):
        rows = pl.ds(base, step)
        for sp in range(CUTOFF):
            for s in range(CUTOFF):
                total = None
                for tp in range(CUTOFF):
                    for t in range(CUTOFF):
                        term = gate_ref[s * CUTOFF + t, sp * CUTOFF + tp] * work_ref[tp, rows, t * width : (t + 1) * width]
                        total = term if total is None else total + term
                high, low = split(total)
                high_ref[sp, rows, s * width : (s + 1) * width] = high
                low_ref[sp, rows, s * width : (s + 1) * width] = low


def project_kernel(members, gate_ref, inverse_ref, sketch_ref, *refs):
    lefts, rights = refs[:members], refs[members : 2 * members]
    out_ref, high_ref, low_ref, work_ref, sum_ref = refs[2 * members :]
    count_p = out_ref.shape[0]
    width = rights[0].shape[2]
    tile = min(width, LANES)
    for s in range(CUTOFF):
        cols = slice(s * count_p, (s + 1) * count_p)
        across = lax.dot_general(
            inverse_ref[...], sketch_ref[:, cols], (((1,), (1,)), ((), ())),
            precision=HIGHEST, preferred_element_type=jnp.float32,
        )
        high_ref[s], low_ref[s] = split(across)
    for m in range(members):
        for s in range(CUTOFF):
            for sp in range(CUTOFF):
                work_ref[s, sp] = dot(high_ref[s], lefts[m][sp]) + dot(low_ref[s], lefts[m][sp])
        for t in range(CUTOFF):
            for tp in range(CUTOFF):
                total = None
                for s in range(CUTOFF):
                    for sp in range(CUTOFF):
                        term = gate_ref[s * CUTOFF + t, sp * CUTOFF + tp] * work_ref[s, sp]
                        total = term if total is None else total + term
                high, low = split(total)
                term = dot(high, rights[m][tp]) + dot(low, rights[m][tp])
                if m == 0 and tp == 0:
                    sum_ref[t] = term
                else:
                    sum_ref[t] += term
    for t in range(CUTOFF):
        for block in range(width // tile):
            base = (block * CUTOFF + t) * tile
            out_ref[:, base : base + tile] = sum_ref[t, :, block * tile : (block + 1) * tile].astype(out_ref.dtype)


def lower_inverse(block):
    factor = jnp.linalg.cholesky(block, symmetrize_input=False)
    return factor, lax.linalg.triangular_solve(
        factor, jnp.eye(block.shape[0], dtype=jnp.float32), left_side=True, lower=True
    )


def inverse_factor(gram):
    half = gram.shape[0] // 2
    _, first = lower_inverse(gram[:half, :half])
    below = jnp.dot(gram[half:, :half], first.T, precision=HIGHEST)
    rest = gram[half:, half:] - jnp.dot(below, below.T, precision=HIGHEST)
    _, second = lower_inverse(rest)
    corner = -jnp.dot(second, jnp.dot(below, first, precision=HIGHEST), precision=HIGHEST)
    return jnp.concatenate(
        [jnp.concatenate([first, jnp.zeros_like(first)], 1), jnp.concatenate([corner, second], 1)], 0
    )


def swap(x, axis):
    return lax.all_to_all(x, axis, split_axis=0, concat_axis=0, tiled=True)


def mate(x, axis, distance):
    return lax.ppermute(x, axis, [(i, i ^ distance) for i in range(lax.axis_size(axis))])


def gather(x, axis):
    return swap(jnp.broadcast_to(x[None], (lax.axis_size(axis),) + x.shape), axis)


def local(left_site, right_site, gate, probes_matrix):
    count_a, _, bond = left_site.shape
    count_c, _, width_b = right_site.shape
    probes = probes_matrix.shape[1]
    rows_n = lax.axis_size("row")
    cols_n = lax.axis_size("col")
    place = lax.axis_index("row")
    vmem = pl.BlockSpec(memory_space=pltpu.VMEM)
    smem = pl.BlockSpec(memory_space=pltpu.SMEM)
    params = pltpu.CompilerParams(vmem_limit_bytes=56 * 1024 * 1024)
    size_q = CUTOFF * probes

    chunks = jnp.transpose(left_site.reshape(count_a, CUTOFF, rows_n, count_c), (2, 1, 0, 3))
    left = swap(chunks, "row")
    left = jnp.transpose(left, (1, 0, 2, 3)).reshape(CUTOFF, rows_n * count_a, count_c)
    right = jnp.transpose(right_site, (1, 0, 2))
    width = width_b // GROUP
    quarter = place % GROUP
    rights = []
    for m in range(GROUP):
        block = lax.dynamic_slice_in_dim(right, (quarter ^ m) * width, width, 2)
        rights.append(mate(block, "row", m) if m else block)
    lefts = [mate(left, "row", m) if m else left for m in range(GROUP)]

    shape = jax.ShapeDtypeStruct((CUTOFF, count_c, size_q), jnp.bfloat16)
    high, low = pl.pallas_call(
        probe_kernel,
        out_shape=(shape, shape),
        in_specs=[smem, vmem, vmem],
        out_specs=(vmem, vmem),
        scratch_shapes=[pltpu.VMEM((CUTOFF, count_c, size_q), jnp.float32)],
        compiler_params=params,
        cost_estimate=pl.CostEstimate(
            flops=2 * CUTOFF * count_c * width_b * size_q, bytes_accessed=10_000_000, transcendentals=0
        ),
    )(gate, right, probes_matrix.reshape(width_b, size_q))

    partial_value = sum(dot(left[sp], high[sp]) + dot(left[sp], low[sp]) for sp in range(CUTOFF))
    piece = partial_value.reshape(-1, cols_n, size_q // cols_n).transpose(1, 0, 2)
    piece = jnp.sum(swap(piece, "col"), 0)
    piece = swap(piece.reshape(rows_n, count_a, -1), "row")
    piece = jnp.sum(piece, 0)
    piece = gather(piece, "row").reshape(rows_n * count_a, -1)
    sketch = gather(piece, "col").transpose(1, 0, 2).reshape(rows_n * count_a, size_q)

    slabs = sketch.reshape(rows_n * count_a, CUTOFF, probes)
    gram = lax.dot_general(slabs, slabs, (((0, 1), (0, 1)), ((), ())), precision=HIGHEST)
    inverse = inverse_factor(gram)

    part = pl.pallas_call(
        functools.partial(project_kernel, GROUP),
        out_shape=jax.ShapeDtypeStruct((probes, CUTOFF * width), jnp.bfloat16),
        in_specs=[smem] + [vmem] * (2 + 2 * GROUP),
        out_specs=vmem,
        scratch_shapes=[
            pltpu.VMEM((CUTOFF, probes, rows_n * count_a), jnp.bfloat16),
            pltpu.VMEM((CUTOFF, probes, rows_n * count_a), jnp.bfloat16),
            pltpu.VMEM((CUTOFF, CUTOFF, probes, count_c), jnp.float32),
            pltpu.VMEM((CUTOFF, probes, width), jnp.float32),
        ],
        compiler_params=params,
        cost_estimate=pl.CostEstimate(
            flops=4 * CUTOFF * count_c * width_b * size_q, bytes_accessed=10_000_000, transcendentals=0
        ),
    )(gate, inverse, sketch, *lefts, *rights)
    own_p = probes // rows_n
    arrived = swap(part.reshape(rows_n, own_p, CUTOFF * width), "row")

    own = lax.dynamic_slice_in_dim(sketch, place * count_a, count_a, 0).reshape(count_a * CUTOFF, probes)
    basis = lax.dot_general(own, inverse, (((1,), (1,)), ((), ())), precision=HIGHEST)

    summed = jnp.sum(arrived.reshape(rows_n // GROUP, GROUP * own_p, -1).astype(jnp.float32), 0)
    tile = min(width, LANES)
    wide = CUTOFF * tile
    source = jnp.arange(wide)
    target = (source % tile) * CUTOFF + source // tile
    order = (target[:, None] == jnp.arange(wide)[None, :]).astype(jnp.float32)
    blocks = jnp.dot(summed.reshape(-1, wide), order, precision=HIGHEST)
    new_block = jnp.transpose(blocks.reshape(GROUP, own_p, -1), (1, 0, 2)).reshape(own_p, -1)
    return (basis, new_block)


def solution(mesh):
    return jax.shard_map(
        local,
        mesh=mesh,
        in_specs=(P("row", None, None), P("row", None, "col"), P(), P("col", None)),
        out_specs=(P("row", None), P("row", "col")),
        check_vma=False,
    )
```

```python
import functools

import jax
import jax.numpy as jnp
from jax import lax
from jax.experimental import pallas as pl
from jax.experimental.pallas import tpu as pltpu
from jax.sharding import PartitionSpec as P

CUTOFF = 3
LANES = 128
GROUP = 4
HIGHEST = lax.Precision.HIGHEST


def dot(a, b, dims=((1,), (0,))):
    return lax.dot_general(a, b, (dims, ((), ())), preferred_element_type=jnp.float32)


def split(x):
    high = x.astype(jnp.bfloat16)
    low = (x - high.astype(jnp.float32)).astype(jnp.bfloat16)
    return high, low


def probe_kernel(gate_ref, right_ref, probes_ref, high_ref, low_ref, work_ref):
    width = probes_ref.shape[1] // CUTOFF
    for inner in range(CUTOFF):
        work_ref[inner] = dot(right_ref[inner], probes_ref[...])
    count_c = right_ref.shape[1]
    step = min(count_c, 64)
    for base in range(0, count_c, step):
        rows = pl.ds(base, step)
        for sp in range(CUTOFF):
            for s in range(CUTOFF):
                total = None
                for tp in range(CUTOFF):
                    for t in range(CUTOFF):
                        term = gate_ref[s * CUTOFF + t, sp * CUTOFF + tp] * work_ref[tp, rows, t * width : (t + 1) * width]
                        total = term if total is None else total + term
                high, low = split(total)
                high_ref[sp, rows, s * width : (s + 1) * width] = high
                low_ref[sp, rows, s * width : (s + 1) * width] = low


def project_kernel(members, gate_ref, inverse_ref, sketch_ref, *refs):
    lefts, rights = refs[:members], refs[members : 2 * members]
    out_ref, high_ref, low_ref, work_ref, sum_ref = refs[2 * members :]
    count_p = out_ref.shape[0]
    width = rights[0].shape[2]
    tile = min(width, LANES)
    for s in range(CUTOFF):
        cols = slice(s * count_p, (s + 1) * count_p)
        across = lax.dot_general(
            inverse_ref[...], sketch_ref[:, cols], (((1,), (1,)), ((), ())),
            precision=HIGHEST, preferred_element_type=jnp.float32,
        )
        high_ref[s], low_ref[s] = split(across)
    for m in range(members):
        for s in range(CUTOFF):
            for sp in range(CUTOFF):
                work_ref[s, sp] = dot(high_ref[s], lefts[m][sp]) + dot(low_ref[s], lefts[m][sp])
        for t in range(CUTOFF):
            for tp in range(CUTOFF):
                total = None
                for s in range(CUTOFF):
                    for sp in range(CUTOFF):
                        term = gate_ref[s * CUTOFF + t, sp * CUTOFF + tp] * work_ref[s, sp]
                        total = term if total is None else total + term
                high, low = split(total)
                term = dot(high, rights[m][tp]) + dot(low, rights[m][tp])
                if m == 0 and tp == 0:
                    sum_ref[t] = term
                else:
                    sum_ref[t] += term
    for t in range(CUTOFF):
        for block in range(width // tile):
            base = (block * CUTOFF + t) * tile
            out_ref[:, base : base + tile] = sum_ref[t, :, block * tile : (block + 1) * tile].astype(out_ref.dtype)


def lower_inverse(block):
    factor = jnp.linalg.cholesky(block, symmetrize_input=False)
    return factor, lax.linalg.triangular_solve(
        factor, jnp.eye(block.shape[0], dtype=jnp.float32), left_side=True, lower=True
    )


def inverse_factor(gram):
    half = gram.shape[0] // 2
    _, first = lower_inverse(gram[:half, :half])
    below = jnp.dot(gram[half:, :half], first.T, precision=HIGHEST)
    rest = gram[half:, half:] - jnp.dot(below, below.T, precision=HIGHEST)
    _, second = lower_inverse(rest)
    corner = -jnp.dot(second, jnp.dot(below, first, precision=HIGHEST), precision=HIGHEST)
    return jnp.concatenate(
        [jnp.concatenate([first, jnp.zeros_like(first)], 1), jnp.concatenate([corner, second], 1)], 0
    )


def total_kernel(part_ref, out_ref, sum_ref, col_ref, row_ref, col_send, col_recv, row_send, row_recv,
                 own_send, own_recv, all_send, all_recv):
    cols_n, rows_n = part_ref.shape[:2]
    row, col = lax.axis_index("row"), lax.axis_index("col")

    def over(source, target, send, recv, axis, peer):
        return pltpu.make_async_remote_copy(
            src_ref=source, dst_ref=target, send_sem=send, recv_sem=recv,
            device_id={axis: peer}, device_id_type=pl.DeviceIdType.MESH,
        )

    row_peers = [(o, lax.rem(row + o, rows_n)) for o in range(1, rows_n)]
    col_peers = [(o, lax.rem(col + o, cols_n)) for o in range(1, cols_n)]
    barrier = pltpu.get_barrier_semaphore()
    for axis, peers in (("row", row_peers), ("col", col_peers)):
        for _, peer in peers:
            pl.semaphore_signal(barrier, inc=1, device_id={axis: peer}, device_id_type=pl.DeviceIdType.MESH)
    pl.semaphore_wait(barrier, rows_n + cols_n - 2)

    copies = [over(part_ref.at[p], col_ref.at[o], col_send.at[o], col_recv.at[o], "col", p) for o, p in col_peers]
    for copy in copies:
        copy.start()
    for copy in copies:
        copy.wait()
    value = part_ref[col]
    for o, _ in col_peers:
        value = value + col_ref[o]
    sum_ref[...] = value

    copies = [over(sum_ref.at[p], row_ref.at[o], row_send.at[o], row_recv.at[o], "row", p) for o, p in row_peers]
    for copy in copies:
        copy.start()
    for copy in copies:
        copy.wait()
    value = sum_ref[row]
    for o, _ in row_peers:
        value = value + row_ref[o]
    out_ref[col, row] = value

    mine = out_ref.at[col, row]
    copies = [over(mine, mine, own_send.at[o], own_recv.at[o], "row", p) for o, p in row_peers]
    for copy in copies:
        copy.start()
    for copy in copies:
        copy.wait()
    mine = out_ref.at[col]
    copies = [over(mine, mine, all_send.at[o], all_recv.at[o], "col", p) for o, p in col_peers]
    for copy in copies:
        copy.start()
    for copy in copies:
        copy.wait()


def swap(x, axis):
    return lax.all_to_all(x, axis, split_axis=0, concat_axis=0, tiled=True)


def mate(x, axis, distance):
    return lax.ppermute(x, axis, [(i, i ^ distance) for i in range(lax.axis_size(axis))])


def local(left_site, right_site, gate, probes_matrix):
    count_a, _, bond = left_site.shape
    count_c, _, width_b = right_site.shape
    probes = probes_matrix.shape[1]
    rows_n = lax.axis_size("row")
    cols_n = lax.axis_size("col")
    place = lax.axis_index("row")
    vmem = pl.BlockSpec(memory_space=pltpu.VMEM)
    smem = pl.BlockSpec(memory_space=pltpu.SMEM)
    params = pltpu.CompilerParams(vmem_limit_bytes=56 * 1024 * 1024)
    size_q = CUTOFF * probes

    chunks = jnp.transpose(left_site.reshape(count_a, CUTOFF, rows_n, count_c), (2, 1, 0, 3))
    left = swap(chunks, "row")
    left = jnp.transpose(left, (1, 0, 2, 3)).reshape(CUTOFF, rows_n * count_a, count_c)
    right = jnp.transpose(right_site, (1, 0, 2))
    width = width_b // GROUP
    quarter = place % GROUP
    rights = []
    for m in range(GROUP):
        block = lax.dynamic_slice_in_dim(right, (quarter ^ m) * width, width, 2)
        rights.append(mate(block, "row", m) if m else block)
    lefts = [mate(left, "row", m) if m else left for m in range(GROUP)]

    shape = jax.ShapeDtypeStruct((CUTOFF, count_c, size_q), jnp.bfloat16)
    high, low = pl.pallas_call(
        probe_kernel,
        out_shape=(shape, shape),
        in_specs=[smem, vmem, vmem],
        out_specs=(vmem, vmem),
        scratch_shapes=[pltpu.VMEM((CUTOFF, count_c, size_q), jnp.float32)],
        compiler_params=params,
        cost_estimate=pl.CostEstimate(
            flops=2 * CUTOFF * count_c * width_b * size_q, bytes_accessed=10_000_000, transcendentals=0
        ),
    )(gate, right, probes_matrix.reshape(width_b, size_q))

    partial_value = sum(dot(left[sp], high[sp]) + dot(left[sp], low[sp]) for sp in range(CUTOFF))
    piece = partial_value.reshape(rows_n, count_a, cols_n, size_q // cols_n).transpose(2, 0, 1, 3)
    dma = pltpu.SemaphoreType.DMA
    total = pl.pallas_call(
        total_kernel,
        out_shape=jax.ShapeDtypeStruct(piece.shape, jnp.float32),
        in_specs=[vmem],
        out_specs=vmem,
        scratch_shapes=[
            pltpu.VMEM(piece.shape[1:], jnp.float32),
            pltpu.VMEM(piece.shape, jnp.float32),
            pltpu.VMEM(piece.shape[1:], jnp.float32),
            dma((cols_n,)), dma((cols_n,)), dma((rows_n,)), dma((rows_n,)),
            dma((rows_n,)), dma((rows_n,)), dma((cols_n,)), dma((cols_n,)),
        ],
        compiler_params=pltpu.CompilerParams(
            collective_id=0, has_side_effects=True, vmem_limit_bytes=56 * 1024 * 1024
        ),
    )(piece)
    sketch = total.transpose(1, 2, 0, 3).reshape(rows_n * count_a, size_q)

    slabs = sketch.reshape(rows_n * count_a, CUTOFF, probes)
    gram = lax.dot_general(slabs, slabs, (((0, 1), (0, 1)), ((), ())), precision=HIGHEST)
    inverse = inverse_factor(gram)

    part = pl.pallas_call(
        functools.partial(project_kernel, GROUP),
        out_shape=jax.ShapeDtypeStruct((probes, CUTOFF * width), jnp.bfloat16),
        in_specs=[smem] + [vmem] * (2 + 2 * GROUP),
        out_specs=vmem,
        scratch_shapes=[
            pltpu.VMEM((CUTOFF, probes, rows_n * count_a), jnp.bfloat16),
            pltpu.VMEM((CUTOFF, probes, rows_n * count_a), jnp.bfloat16),
            pltpu.VMEM((CUTOFF, CUTOFF, probes, count_c), jnp.float32),
            pltpu.VMEM((CUTOFF, probes, width), jnp.float32),
        ],
        compiler_params=params,
        cost_estimate=pl.CostEstimate(
            flops=4 * CUTOFF * count_c * width_b * size_q, bytes_accessed=10_000_000, transcendentals=0
        ),
    )(gate, inverse, sketch, *lefts, *rights)
    own_p = probes // rows_n
    arrived = swap(part.reshape(rows_n, own_p, CUTOFF * width), "row")

    own = lax.dynamic_slice_in_dim(sketch, place * count_a, count_a, 0).reshape(count_a * CUTOFF, probes)
    basis = lax.dot_general(own, inverse, (((1,), (1,)), ((), ())), precision=HIGHEST)

    summed = jnp.sum(arrived.reshape(rows_n // GROUP, GROUP * own_p, -1).astype(jnp.float32), 0)
    tile = min(width, LANES)
    wide = CUTOFF * tile
    source = jnp.arange(wide)
    target = (source % tile) * CUTOFF + source // tile
    order = (target[:, None] == jnp.arange(wide)[None, :]).astype(jnp.float32)
    blocks = jnp.dot(summed.reshape(-1, wide), order, precision=HIGHEST)
    new_block = jnp.transpose(blocks.reshape(GROUP, own_p, -1), (1, 0, 2)).reshape(own_p, -1)
    return (basis, new_block)


def solution(mesh):
    return jax.shard_map(
        local,
        mesh=mesh,
        in_specs=(P("row", None, None), P("row", None, "col"), P(), P("col", None)),
        out_specs=(P("row", None), P("row", "col")),
        check_vma=False,
    )
```

```python
import functools

import jax
import jax.numpy as jnp
from jax import lax
from jax.experimental import pallas as pl
from jax.experimental.pallas import tpu as pltpu
from jax.sharding import PartitionSpec as P

CUTOFF = 3
LANES = 128
GROUP = 4
HIGHEST = lax.Precision.HIGHEST


def dot(a, b, dims=((1,), (0,))):
    return lax.dot_general(a, b, (dims, ((), ())), preferred_element_type=jnp.float32)


def split(x):
    high = x.astype(jnp.bfloat16)
    low = (x - high.astype(jnp.float32)).astype(jnp.bfloat16)
    return high, low


def probe_kernel(gate_ref, right_ref, probes_ref, high_ref, low_ref, work_ref):
    width = probes_ref.shape[1] // CUTOFF
    for inner in range(CUTOFF):
        work_ref[inner] = dot(right_ref[inner], probes_ref[...])
    count_c = right_ref.shape[1]
    step = min(count_c, 64)
    for base in range(0, count_c, step):
        rows = pl.ds(base, step)
        for sp in range(CUTOFF):
            for s in range(CUTOFF):
                total = None
                for tp in range(CUTOFF):
                    for t in range(CUTOFF):
                        term = gate_ref[s * CUTOFF + t, sp * CUTOFF + tp] * work_ref[tp, rows, t * width : (t + 1) * width]
                        total = term if total is None else total + term
                high, low = split(total)
                high_ref[sp, rows, s * width : (s + 1) * width] = high
                low_ref[sp, rows, s * width : (s + 1) * width] = low


def project_kernel(members, gate_ref, inverse_ref, sketch_ref, *refs):
    lefts, rights = refs[:members], refs[members : 2 * members]
    out_ref, high_ref, low_ref, work_ref, sum_ref = refs[2 * members :]
    count_p = out_ref.shape[0]
    width = rights[0].shape[2]
    tile = min(width, LANES)
    for s in range(CUTOFF):
        cols = slice(s * count_p, (s + 1) * count_p)
        across = lax.dot_general(
            inverse_ref[...], sketch_ref[:, cols], (((1,), (1,)), ((), ())),
            precision=HIGHEST, preferred_element_type=jnp.float32,
        )
        high_ref[s], low_ref[s] = split(across)
    for m in range(members):
        for s in range(CUTOFF):
            for sp in range(CUTOFF):
                work_ref[s, sp] = dot(high_ref[s], lefts[m][sp]) + dot(low_ref[s], lefts[m][sp])
        for t in range(CUTOFF):
            for tp in range(CUTOFF):
                total = None
                for s in range(CUTOFF):
                    for sp in range(CUTOFF):
                        term = gate_ref[s * CUTOFF + t, sp * CUTOFF + tp] * work_ref[s, sp]
                        total = term if total is None else total + term
                high, low = split(total)
                term = dot(high, rights[m][tp]) + dot(low, rights[m][tp])
                if m == 0 and tp == 0:
                    sum_ref[t] = term
                else:
                    sum_ref[t] += term
    for t in range(CUTOFF):
        for block in range(width // tile):
            base = (block * CUTOFF + t) * tile
            out_ref[:, base : base + tile] = sum_ref[t, :, block * tile : (block + 1) * tile].astype(out_ref.dtype)


def lower_inverse(block):
    factor = jnp.linalg.cholesky(block, symmetrize_input=False)
    return factor, lax.linalg.triangular_solve(
        factor, jnp.eye(block.shape[0], dtype=jnp.float32), left_side=True, lower=True
    )


def inverse_factor(gram):
    half = gram.shape[0] // 2
    _, first = lower_inverse(gram[:half, :half])
    below = jnp.dot(gram[half:, :half], first.T, precision=HIGHEST)
    rest = gram[half:, half:] - jnp.dot(below, below.T, precision=HIGHEST)
    _, second = lower_inverse(rest)
    corner = -jnp.dot(second, jnp.dot(below, first, precision=HIGHEST), precision=HIGHEST)
    return jnp.concatenate(
        [jnp.concatenate([first, jnp.zeros_like(first)], 1), jnp.concatenate([corner, second], 1)], 0
    )


def total_kernel(part_ref, out_ref, sum_ref, col_ref, row_ref, col_send, col_recv, row_send, row_recv,
                 own_send, own_recv, all_send, all_recv):
    cols_n, rows_n = part_ref.shape[:2]
    row, col = lax.axis_index("row"), lax.axis_index("col")

    def over(source, target, send, recv, axis, peer):
        return pltpu.make_async_remote_copy(
            src_ref=source, dst_ref=target, send_sem=send, recv_sem=recv,
            device_id={axis: peer}, device_id_type=pl.DeviceIdType.MESH,
        )

    row_peers = [(o, lax.rem(row + o, rows_n)) for o in range(1, rows_n)]
    col_peers = [(o, lax.rem(col + o, cols_n)) for o in range(1, cols_n)]
    barrier = pltpu.get_barrier_semaphore()
    for axis, peers in (("row", row_peers), ("col", col_peers)):
        for _, peer in peers:
            pl.semaphore_signal(barrier, inc=1, device_id={axis: peer}, device_id_type=pl.DeviceIdType.MESH)
    pl.semaphore_wait(barrier, rows_n + cols_n - 2)

    copies = [over(part_ref.at[p], col_ref.at[o], col_send.at[o], col_recv.at[o], "col", p) for o, p in col_peers]
    for copy in copies:
        copy.start()
    for copy in copies:
        copy.wait()
    value = part_ref[col]
    for o, _ in col_peers:
        value = value + col_ref[o]
    sum_ref[...] = value

    copies = [over(sum_ref.at[p], row_ref.at[o], row_send.at[o], row_recv.at[o], "row", p) for o, p in row_peers]
    for copy in copies:
        copy.start()
    for copy in copies:
        copy.wait()
    value = sum_ref[row]
    for o, _ in row_peers:
        value = value + row_ref[o]
    out_ref[col, row] = value

    mine = out_ref.at[col, row]
    copies = [over(mine, mine, own_send.at[o], own_recv.at[o], "row", p) for o, p in row_peers]
    for copy in copies:
        copy.start()
    for copy in copies:
        copy.wait()
    mine = out_ref.at[col]
    copies = [over(mine, mine, all_send.at[o], all_recv.at[o], "col", p) for o, p in col_peers]
    for copy in copies:
        copy.start()
    for copy in copies:
        copy.wait()


def swap(x, axis):
    return lax.all_to_all(x, axis, split_axis=0, concat_axis=0, tiled=True)


def mate(x, axis, distance):
    return lax.ppermute(x, axis, [(i, i ^ distance) for i in range(lax.axis_size(axis))])


def local(left_site, right_site, gate, probes_matrix):
    count_a, _, bond = left_site.shape
    count_c, _, width_b = right_site.shape
    probes = probes_matrix.shape[1]
    rows_n = lax.axis_size("row")
    cols_n = lax.axis_size("col")
    place = lax.axis_index("row")
    vmem = pl.BlockSpec(memory_space=pltpu.VMEM)
    smem = pl.BlockSpec(memory_space=pltpu.SMEM)
    params = pltpu.CompilerParams(vmem_limit_bytes=56 * 1024 * 1024)
    size_q = CUTOFF * probes

    chunks = jnp.transpose(left_site.reshape(count_a, CUTOFF, rows_n, count_c), (2, 1, 0, 3))
    left = swap(chunks, "row")
    left = jnp.transpose(left, (1, 0, 2, 3)).reshape(CUTOFF, rows_n * count_a, count_c)
    right = jnp.transpose(right_site, (1, 0, 2))
    width = width_b // GROUP
    quarter = place % GROUP
    rights = []
    for m in range(GROUP):
        block = lax.dynamic_slice_in_dim(right, (quarter ^ m) * width, width, 2)
        rights.append(mate(block, "row", m) if m else block)

    shape = jax.ShapeDtypeStruct((CUTOFF, count_c, size_q), jnp.bfloat16)
    high, low = pl.pallas_call(
        probe_kernel,
        out_shape=(shape, shape),
        in_specs=[smem, vmem, vmem],
        out_specs=(vmem, vmem),
        scratch_shapes=[pltpu.VMEM((CUTOFF, count_c, size_q), jnp.float32)],
        compiler_params=params,
        cost_estimate=pl.CostEstimate(
            flops=2 * CUTOFF * count_c * width_b * size_q, bytes_accessed=10_000_000, transcendentals=0
        ),
    )(gate, right, probes_matrix.reshape(width_b, size_q))

    partial_value = sum(dot(left[sp], high[sp]) + dot(left[sp], low[sp]) for sp in range(CUTOFF))
    piece = partial_value.reshape(rows_n, count_a, cols_n, size_q // cols_n).transpose(2, 0, 1, 3)
    dma = pltpu.SemaphoreType.DMA
    total = pl.pallas_call(
        total_kernel,
        out_shape=jax.ShapeDtypeStruct(piece.shape, jnp.float32),
        in_specs=[vmem],
        out_specs=vmem,
        scratch_shapes=[
            pltpu.VMEM(piece.shape[1:], jnp.float32),
            pltpu.VMEM(piece.shape, jnp.float32),
            pltpu.VMEM(piece.shape[1:], jnp.float32),
            dma((cols_n,)), dma((cols_n,)), dma((rows_n,)), dma((rows_n,)),
            dma((rows_n,)), dma((rows_n,)), dma((cols_n,)), dma((cols_n,)),
        ],
        compiler_params=pltpu.CompilerParams(
            collective_id=0, has_side_effects=True, vmem_limit_bytes=56 * 1024 * 1024
        ),
    )(piece)
    late, total = lax.optimization_barrier((left, total))
    lefts = [mate(late, "row", m) if m else late for m in range(GROUP)]
    sketch = total.transpose(1, 2, 0, 3).reshape(rows_n * count_a, size_q)

    slabs = sketch.reshape(rows_n * count_a, CUTOFF, probes)
    gram = lax.dot_general(slabs, slabs, (((0, 1), (0, 1)), ((), ())), precision=HIGHEST)
    inverse = inverse_factor(gram)

    part = pl.pallas_call(
        functools.partial(project_kernel, GROUP),
        out_shape=jax.ShapeDtypeStruct((probes, CUTOFF * width), jnp.bfloat16),
        in_specs=[smem] + [vmem] * (2 + 2 * GROUP),
        out_specs=vmem,
        scratch_shapes=[
            pltpu.VMEM((CUTOFF, probes, rows_n * count_a), jnp.bfloat16),
            pltpu.VMEM((CUTOFF, probes, rows_n * count_a), jnp.bfloat16),
            pltpu.VMEM((CUTOFF, CUTOFF, probes, count_c), jnp.float32),
            pltpu.VMEM((CUTOFF, probes, width), jnp.float32),
        ],
        compiler_params=params,
        cost_estimate=pl.CostEstimate(
            flops=4 * CUTOFF * count_c * width_b * size_q, bytes_accessed=10_000_000, transcendentals=0
        ),
    )(gate, inverse, sketch, *lefts, *rights)
    own_p = probes // rows_n
    arrived = swap(part.reshape(rows_n, own_p, CUTOFF * width), "row")

    own = lax.dynamic_slice_in_dim(sketch, place * count_a, count_a, 0).reshape(count_a * CUTOFF, probes)
    basis = lax.dot_general(own, inverse, (((1,), (1,)), ((), ())), precision=HIGHEST)

    summed = jnp.sum(arrived.reshape(rows_n // GROUP, GROUP * own_p, -1).astype(jnp.float32), 0)
    tile = min(width, LANES)
    wide = CUTOFF * tile
    source = jnp.arange(wide)
    target = (source % tile) * CUTOFF + source // tile
    order = (target[:, None] == jnp.arange(wide)[None, :]).astype(jnp.float32)
    blocks = jnp.dot(summed.reshape(-1, wide), order, precision=HIGHEST)
    new_block = jnp.transpose(blocks.reshape(GROUP, own_p, -1), (1, 0, 2)).reshape(own_p, -1)
    return (basis, new_block)


def solution(mesh):
    return jax.shard_map(
        local,
        mesh=mesh,
        in_specs=(P("row", None, None), P("row", None, "col"), P(), P("col", None)),
        out_specs=(P("row", None), P("row", "col")),
        check_vma=False,
    )
```

```python
import functools

import jax
import jax.numpy as jnp
from jax import lax
from jax.experimental import pallas as pl
from jax.experimental.pallas import tpu as pltpu
from jax.sharding import PartitionSpec as P

CUTOFF = 3
LANES = 128
GROUP = 4
HIGHEST = lax.Precision.HIGHEST


def dot(a, b, dims=((1,), (0,))):
    return lax.dot_general(a, b, (dims, ((), ())), preferred_element_type=jnp.float32)


def split(x):
    high = x.astype(jnp.bfloat16)
    low = (x - high.astype(jnp.float32)).astype(jnp.bfloat16)
    return high, low


def probe_kernel(gate_ref, right_ref, probes_ref, high_ref, low_ref, work_ref):
    width = probes_ref.shape[1] // CUTOFF
    for inner in range(CUTOFF):
        work_ref[inner] = dot(right_ref[inner], probes_ref[...])
    count_c = right_ref.shape[1]
    step = min(count_c, 64)
    for base in range(0, count_c, step):
        rows = pl.ds(base, step)
        for sp in range(CUTOFF):
            for s in range(CUTOFF):
                total = None
                for tp in range(CUTOFF):
                    for t in range(CUTOFF):
                        term = gate_ref[s * CUTOFF + t, sp * CUTOFF + tp] * work_ref[tp, rows, t * width : (t + 1) * width]
                        total = term if total is None else total + term
                high, low = split(total)
                high_ref[sp, rows, s * width : (s + 1) * width] = high
                low_ref[sp, rows, s * width : (s + 1) * width] = low


def project_kernel(members, gate_ref, inverse_ref, sketch_ref, *refs):
    lefts, rights = refs[:members], refs[members : 2 * members]
    out_ref, high_ref, low_ref, work_ref, sum_ref = refs[2 * members :]
    count_p = out_ref.shape[0]
    width = rights[0].shape[2]
    tile = min(width, LANES)
    for s in range(CUTOFF):
        cols = slice(s * count_p, (s + 1) * count_p)
        across = lax.dot_general(
            inverse_ref[...], sketch_ref[:, cols], (((1,), (1,)), ((), ())),
            precision=HIGHEST, preferred_element_type=jnp.float32,
        )
        high_ref[s], low_ref[s] = split(across)
    for m in range(members):
        for s in range(CUTOFF):
            for sp in range(CUTOFF):
                work_ref[s, sp] = dot(high_ref[s], lefts[m][sp]) + dot(low_ref[s], lefts[m][sp])
        for t in range(CUTOFF):
            for tp in range(CUTOFF):
                total = None
                for s in range(CUTOFF):
                    for sp in range(CUTOFF):
                        term = gate_ref[s * CUTOFF + t, sp * CUTOFF + tp] * work_ref[s, sp]
                        total = term if total is None else total + term
                high, low = split(total)
                term = dot(high, rights[m][tp]) + dot(low, rights[m][tp])
                if m == 0 and tp == 0:
                    sum_ref[t] = term
                else:
                    sum_ref[t] += term
    for t in range(CUTOFF):
        for block in range(width // tile):
            base = (block * CUTOFF + t) * tile
            out_ref[:, base : base + tile] = sum_ref[t, :, block * tile : (block + 1) * tile].astype(out_ref.dtype)


def lower_inverse(block):
    factor = jnp.linalg.cholesky(block, symmetrize_input=False)
    return factor, lax.linalg.triangular_solve(
        factor, jnp.eye(block.shape[0], dtype=jnp.float32), left_side=True, lower=True
    )


def inverse_factor(gram):
    half = gram.shape[0] // 2
    _, first = lower_inverse(gram[:half, :half])
    below = jnp.dot(gram[half:, :half], first.T, precision=HIGHEST)
    rest = gram[half:, half:] - jnp.dot(below, below.T, precision=HIGHEST)
    _, second = lower_inverse(rest)
    corner = -jnp.dot(second, jnp.dot(below, first, precision=HIGHEST), precision=HIGHEST)
    return jnp.concatenate(
        [jnp.concatenate([first, jnp.zeros_like(first)], 1), jnp.concatenate([corner, second], 1)], 0
    )


def total_kernel(part_ref, out_ref, sum_ref, col_ref, row_ref, col_send, col_recv, row_send, row_recv,
                 own_send, own_recv, all_send, all_recv):
    cols_n, rows_n = part_ref.shape[:2]
    row, col = lax.axis_index("row"), lax.axis_index("col")

    def over(source, target, send, recv, axis, peer):
        return pltpu.make_async_remote_copy(
            src_ref=source, dst_ref=target, send_sem=send, recv_sem=recv,
            device_id={axis: peer}, device_id_type=pl.DeviceIdType.MESH,
        )

    row_peers = [(o, lax.rem(row + o, rows_n)) for o in range(1, rows_n)]
    col_peers = [(o, lax.rem(col + o, cols_n)) for o in range(1, cols_n)]
    barrier = pltpu.get_barrier_semaphore()
    for axis, peers in (("row", row_peers), ("col", col_peers)):
        for _, peer in peers:
            pl.semaphore_signal(barrier, inc=1, device_id={axis: peer}, device_id_type=pl.DeviceIdType.MESH)
    pl.semaphore_wait(barrier, rows_n + cols_n - 2)

    copies = [over(part_ref.at[p], col_ref.at[o], col_send.at[o], col_recv.at[o], "col", p) for o, p in col_peers]
    for copy in copies:
        copy.start()
    for copy in copies:
        copy.wait()
    value = part_ref[col]
    for o, _ in col_peers:
        value = value + col_ref[o]
    sum_ref[...] = value

    copies = [over(sum_ref.at[p], row_ref.at[o], row_send.at[o], row_recv.at[o], "row", p) for o, p in row_peers]
    for copy in copies:
        copy.start()
    for copy in copies:
        copy.wait()
    value = sum_ref[row]
    for o, _ in row_peers:
        value = value + row_ref[o]
    out_ref[col, row] = value

    mine = out_ref.at[col, row]
    copies = [over(mine, mine, own_send.at[o], own_recv.at[o], "row", p) for o, p in row_peers]
    for copy in copies:
        copy.start()
    for copy in copies:
        copy.wait()
    mine = out_ref.at[col]
    copies = [over(mine, mine, all_send.at[o], all_recv.at[o], "col", p) for o, p in col_peers]
    for copy in copies:
        copy.start()
    for copy in copies:
        copy.wait()


def swap(x, axis):
    return lax.all_to_all(x, axis, split_axis=0, concat_axis=0, tiled=True)


def mate(x, axis, distance):
    return lax.ppermute(x, axis, [(i, i ^ distance) for i in range(lax.axis_size(axis))])


def local(left_site, right_site, gate, probes_matrix):
    count_a, _, bond = left_site.shape
    count_c, _, width_b = right_site.shape
    probes = probes_matrix.shape[1]
    rows_n = lax.axis_size("row")
    cols_n = lax.axis_size("col")
    place = lax.axis_index("row")
    vmem = pl.BlockSpec(memory_space=pltpu.VMEM)
    smem = pl.BlockSpec(memory_space=pltpu.SMEM)
    params = pltpu.CompilerParams(vmem_limit_bytes=56 * 1024 * 1024)
    size_q = CUTOFF * probes

    chunks = jnp.transpose(left_site.reshape(count_a, CUTOFF, rows_n, count_c), (2, 1, 0, 3))
    left = swap(chunks, "row")
    left = jnp.transpose(left, (1, 0, 2, 3)).reshape(CUTOFF, rows_n * count_a, count_c)
    right = jnp.transpose(right_site, (1, 0, 2))
    width = width_b // GROUP
    quarter = place % GROUP
    rights = []
    for m in range(GROUP):
        block = lax.dynamic_slice_in_dim(right, (quarter ^ m) * width, width, 2)
        rights.append(block)

    shape = jax.ShapeDtypeStruct((CUTOFF, count_c, size_q), jnp.bfloat16)
    high, low = pl.pallas_call(
        probe_kernel,
        out_shape=(shape, shape),
        in_specs=[smem, vmem, vmem],
        out_specs=(vmem, vmem),
        scratch_shapes=[pltpu.VMEM((CUTOFF, count_c, size_q), jnp.float32)],
        compiler_params=params,
        cost_estimate=pl.CostEstimate(
            flops=2 * CUTOFF * count_c * width_b * size_q, bytes_accessed=10_000_000, transcendentals=0
        ),
    )(gate, right, probes_matrix.reshape(width_b, size_q))

    partial_value = sum(dot(left[sp], high[sp]) + dot(left[sp], low[sp]) for sp in range(CUTOFF))
    piece = partial_value.reshape(rows_n, count_a, cols_n, size_q // cols_n).transpose(2, 0, 1, 3)
    dma = pltpu.SemaphoreType.DMA
    total = pl.pallas_call(
        total_kernel,
        out_shape=jax.ShapeDtypeStruct(piece.shape, jnp.float32),
        in_specs=[vmem],
        out_specs=vmem,
        scratch_shapes=[
            pltpu.VMEM(piece.shape[1:], jnp.float32),
            pltpu.VMEM(piece.shape, jnp.float32),
            pltpu.VMEM(piece.shape[1:], jnp.float32),
            dma((cols_n,)), dma((cols_n,)), dma((rows_n,)), dma((rows_n,)),
            dma((rows_n,)), dma((rows_n,)), dma((cols_n,)), dma((cols_n,)),
        ],
        compiler_params=pltpu.CompilerParams(
            collective_id=0, has_side_effects=True, vmem_limit_bytes=56 * 1024 * 1024
        ),
    )(piece)
    late, rights, total = lax.optimization_barrier((left, rights, total))
    rights = [mate(rights[m], "row", m) if m else rights[m] for m in range(GROUP)]
    lefts = [mate(late, "row", m) if m else late for m in range(GROUP)]
    sketch = total.transpose(1, 2, 0, 3).reshape(rows_n * count_a, size_q)

    slabs = sketch.reshape(rows_n * count_a, CUTOFF, probes)
    gram = lax.dot_general(slabs, slabs, (((0, 1), (0, 1)), ((), ())), precision=HIGHEST)
    inverse = inverse_factor(gram)

    part = pl.pallas_call(
        functools.partial(project_kernel, GROUP),
        out_shape=jax.ShapeDtypeStruct((probes, CUTOFF * width), jnp.bfloat16),
        in_specs=[smem] + [vmem] * (2 + 2 * GROUP),
        out_specs=vmem,
        scratch_shapes=[
            pltpu.VMEM((CUTOFF, probes, rows_n * count_a), jnp.bfloat16),
            pltpu.VMEM((CUTOFF, probes, rows_n * count_a), jnp.bfloat16),
            pltpu.VMEM((CUTOFF, CUTOFF, probes, count_c), jnp.float32),
            pltpu.VMEM((CUTOFF, probes, width), jnp.float32),
        ],
        compiler_params=params,
        cost_estimate=pl.CostEstimate(
            flops=4 * CUTOFF * count_c * width_b * size_q, bytes_accessed=10_000_000, transcendentals=0
        ),
    )(gate, inverse, sketch, *lefts, *rights)
    own_p = probes // rows_n
    arrived = swap(part.reshape(rows_n, own_p, CUTOFF * width), "row")

    own = lax.dynamic_slice_in_dim(sketch, place * count_a, count_a, 0).reshape(count_a * CUTOFF, probes)
    basis = lax.dot_general(own, inverse, (((1,), (1,)), ((), ())), precision=HIGHEST)

    summed = jnp.sum(arrived.reshape(rows_n // GROUP, GROUP * own_p, -1).astype(jnp.float32), 0)
    tile = min(width, LANES)
    wide = CUTOFF * tile
    source = jnp.arange(wide)
    target = (source % tile) * CUTOFF + source // tile
    order = (target[:, None] == jnp.arange(wide)[None, :]).astype(jnp.float32)
    blocks = jnp.dot(summed.reshape(-1, wide), order, precision=HIGHEST)
    new_block = jnp.transpose(blocks.reshape(GROUP, own_p, -1), (1, 0, 2)).reshape(own_p, -1)
    return (basis, new_block)


def solution(mesh):
    return jax.shard_map(
        local,
        mesh=mesh,
        in_specs=(P("row", None, None), P("row", None, "col"), P(), P("col", None)),
        out_specs=(P("row", None), P("row", "col")),
        check_vma=False,
    )
```
